32 devices in a mesh: rep: 8 (over y, x, core), own: 4 (over z).
Axes of the slice: x: 2, y: 2, z: 4, core: 2. Of those that a mesh axis runs over, the one named last changes fastest.
Arguments:
- gradients: bfloat16 [8, 4, 4, 256, 256], P('rep', 'own')
- owner_index: int32 [4], replicated, may hold values from 0 to 3, as said below
- left_stats: float32 [8, 256, 256], P('own'), as said below
- right_stats: float32 [8, 256, 256], P('own'), as said below
- left_roots: bfloat16 [8, 256, 256], P('own'), as said below
- right_roots: bfloat16 [8, 256, 256], P('own'), as said below
- first_moment: float32 [8, 256, 256], P('own')
- second_moment: float32 [8, 256, 256], P('own'), may hold values from 0.05 to 5
- master: float32 [8, 256, 256], P('own'), may hold values from -6 to 6
Outputs:
- new_left: float32 [8, 256, 256], P('own')
- new_right: float32 [8, 256, 256], P('own')
- new_first: float32 [8, 256, 256], P('own')
- new_second: float32 [8, 256, 256], P('own')
- weights: bfloat16 [4, 256, 256], P(None, 'rep')
The draws below stay inside these ranges and needn't reach their ends.
Inputs may be any that keep to these rules, and one draw needn't show every extreme that they name: `owner_index`: exactly one owner holds 2 blocks, exactly one holds none, every other holds one. `left_stats`: each matrix is symmetric; every diagonal entry exceeds the sum of the magnitudes of the other entries of its row. `right_stats`: each matrix is symmetric; every diagonal entry exceeds the sum of the magnitudes of the other entries of its row. `left_roots`: each matrix is symmetric. `right_roots`: each matrix is symmetric.
All inputs are finite; a program needn't handle non-finite values.
Results may differ from the reference program's by a relative error of at most 0.001.
Values may be sent and summed in bfloat16 or wider, within the bound.
A program may use at most 64 MiB of HBM per device.

```python
import math
import jax
import jax.numpy as jnp
from jax import lax

BS = 256
CAP = 2
NEWTON = 4
NBLK = 4
SLOTS = 8
N_REP = 8
N_OWN = 4


def log_scales(key, shape):
    return jnp.exp(jax.random.uniform(key, shape, jnp.float32, -1.15, 1.15))


def mirror_upper(values):
    rows_index = jnp.arange(BS, dtype=jnp.int32)[:, None]
    columns_index = jnp.arange(BS, dtype=jnp.int32)[None, :]
    return jnp.where(rows_index < columns_index, values, jnp.swapaxes(values, 1, 2))


def draw_gradients(key, part):
    subkeys = jax.random.split(jax.random.fold_in(key, 3), 3)
    devices = N_REP * N_OWN
    row_scale = log_scales(subkeys[0], (NBLK, BS, 1))
    column_scale = log_scales(subkeys[1], (NBLK, 1, BS))
    values = jax.random.normal(subkeys[2], (N_REP, N_OWN, NBLK, BS, BS), jnp.float32) / math.sqrt(devices)
    return (values * row_scale * column_scale).astype(jnp.bfloat16)


def draw_owner_index(key, part):
    subkeys = jax.random.split(jax.random.fold_in(key, 7), 3)
    base_owner = jax.random.permutation(subkeys[0], N_OWN).astype(jnp.int32)
    heavy = jax.random.randint(subkeys[1], (), 0, N_OWN, dtype=jnp.int32)
    light = (heavy + jax.random.randint(subkeys[2], (), 1, N_OWN, dtype=jnp.int32)) % N_OWN
    return jnp.where(base_owner == light, heavy, base_owner).astype(jnp.int32)


def statistic_draw(key, variant):
    subkeys = jax.random.split(jax.random.fold_in(key, variant), 3)
    count = N_OWN * CAP
    diagonal = jnp.exp(jax.random.uniform(subkeys[0], (count, BS), jnp.float32, math.log(1.0), math.log(3.0)))
    magnitude = jax.random.uniform(subkeys[1], (count, BS, BS), jnp.float32, 0.5, 0.95) / BS
    signs = jnp.where(jax.random.bernoulli(subkeys[2], 0.5, (count, BS, BS)), 1.0, -1.0)
    mirrored = mirror_upper(magnitude * signs)
    identity = jnp.eye(BS, dtype=jnp.float32)
    return identity[None] * diagonal[:, :, None] + (1.0 - identity[None]) * mirrored


def root_draw(key, variant):
    count = N_OWN * CAP
    amplitude = 0.17 / math.sqrt(BS)
    values = jax.random.uniform(jax.random.fold_in(key, variant), (count, BS, BS), jnp.float32, -amplitude, amplitude)
    identity = jnp.eye(BS, dtype=jnp.float32)
    return (identity[None] + (1.0 - identity[None]) * mirror_upper(values)) * 5.0 ** (-0.25)


def draw_left_stats(key, part):
    return statistic_draw(key, 11)


def draw_right_stats(key, part):
    return statistic_draw(key, 12)


def draw_left_roots(key, part):
    return root_draw(key, 21).astype(jnp.bfloat16)


def draw_right_roots(key, part):
    return root_draw(key, 22).astype(jnp.bfloat16)


def draw_first_moment(key, part):
    subkeys = jax.random.split(jax.random.fold_in(key, 31), 3)
    count = N_OWN * CAP
    row_scale = log_scales(subkeys[0], (count, BS, 1))
    column_scale = log_scales(subkeys[1], (count, 1, BS))
    values = jax.random.normal(subkeys[2], (count, BS, BS), jnp.float32)
    return values * row_scale * column_scale


def shard_levels(key, dims, shards, low, high):
    def one(axis_at, shards_of):
        heights = jax.random.uniform(jax.random.fold_in(jax.random.fold_in(key, 6), axis_at), (shards_of,), jnp.float32, low / len(shards), high / len(shards))
        return jnp.repeat(jnp.exp(heights), dims[axis_at] // shards_of).reshape((-1,) + (1,) * (len(dims) - axis_at - 1))

    loudness = one(*shards[0])
    for cut in shards[1:]:
        loudness = loudness * one(*cut)
    return loudness


def centred(own_key, dims, deviation, reach, pieces=(), kind=jnp.bfloat16):
    drawn = deviation * jax.random.normal(own_key, dims, jnp.float32)
    if pieces:
        drawn = drawn * shard_levels(own_key, dims, pieces, -0.22, 0.18)
    return jnp.clip(drawn, -reach, reach).astype(kind)


def setup_inputs(seed: int = 0) -> dict:
    keys = jax.random.split(jax.random.key(seed), 10)
    gradients = draw_gradients(jax.random.fold_in(keys[9], 71), 0)
    owner_index = draw_owner_index(jax.random.fold_in(keys[9], 71), 0)
    left_stats = draw_left_stats(jax.random.fold_in(keys[9], 71), 0)
    right_stats = draw_right_stats(jax.random.fold_in(keys[9], 71), 0)
    left_roots = draw_left_roots(jax.random.fold_in(keys[9], 71), 0)
    right_roots = draw_right_roots(jax.random.fold_in(keys[9], 71), 0)
    first_moment = draw_first_moment(jax.random.fold_in(keys[9], 71), 0)
    second_moment = jnp.clip(jnp.exp(math.log(5.0) - 4.6051702 * jax.random.uniform(keys[7], (SLOTS, BS, BS), jnp.float32) ** shard_levels(keys[7], (SLOTS, BS, BS), ((0, 4),), -0.2, 0.2)), 0.05, 5.0)
    master = centred(keys[8], (SLOTS, BS, BS), 1.0, 6.0, ((0, 4),), jnp.float32)
    return dict(gradients=gradients, owner_index=owner_index, left_stats=left_stats, right_stats=right_stats, left_roots=left_roots, right_roots=right_roots, first_moment=first_moment, second_moment=second_moment, master=master)


stat_decay = 0.95
first_decay = 0.9
second_decay = 0.99
learning_rate = 0.5

def product(first_factor, second_factor):
    return jnp.matmul(first_factor, second_factor, precision=lax.Precision.HIGHEST)

def destinations(owner_index, capacity):
    block_count = owner_index.shape[0]
    positions = jnp.arange(block_count, dtype=jnp.int32)
    same_owner = owner_index[:, None] == owner_index[None, :]
    earlier = positions[None, :] < positions[:, None]
    ranking = lax.optimization_barrier(jnp.sum((same_owner & earlier).astype(jnp.int32), axis=1)).astype(jnp.int32)
    return (owner_index.astype(jnp.int32) * capacity + ranking).astype(jnp.int32)

def inverse_root(statistic, initial):
    current = initial
    for iteration in range(NEWTON):
        square = product(current, current)
        fourth = product(square, square)
        residual = product(fourth, statistic)
        current = (5.0 * current - product(current, residual)) / 4.0
    return current

def reference(gradients, owner_index, left_stats, right_stats, left_roots, right_roots, first_moment, second_moment, master):
    destination = destinations(owner_index, CAP)
    summed = lax.optimization_barrier(jnp.sum(gradients, axis=(0, 1), dtype=jnp.float32))
    transposed = jnp.swapaxes(summed, 1, 2)
    left_new = stat_decay * left_stats[destination] + (1.0 - stat_decay) / BS * product(summed, transposed)
    right_new = stat_decay * right_stats[destination] + (1.0 - stat_decay) / BS * product(transposed, summed)
    left_root = inverse_root(left_new, left_roots[destination].astype(jnp.float32))
    right_root = inverse_root(right_new, right_roots[destination].astype(jnp.float32))
    first_new = first_decay * first_moment[destination] + (1.0 - first_decay) * summed
    second_new = second_decay * second_moment[destination] + (1.0 - second_decay) * summed * summed
    adam_step = first_new / (jnp.sqrt(second_new) + 1e-08)
    precond = product(product(left_root, summed), right_root)
    graft = jnp.sqrt(lax.optimization_barrier(jnp.sum(adam_step * adam_step, axis=(1, 2)))) / (jnp.sqrt(lax.optimization_barrier(jnp.sum(precond * precond, axis=(1, 2)))) + 1e-06)
    weights = (master[destination] - learning_rate * graft[:, None, None] * precond).astype(jnp.bfloat16)
    new_left = left_stats.at[destination].set(left_new)
    new_right = right_stats.at[destination].set(right_new)
    new_first = first_moment.at[destination].set(first_new)
    new_second = second_moment.at[destination].set(second_new)
    return (new_left, new_right, new_first, new_second, weights)
```

```python
import functools

import jax
import jax.numpy as jnp
from jax import lax
from jax.experimental import pallas as pl
from jax.experimental.pallas import tpu as pltpu
from jax.sharding import PartitionSpec as P

NEWTON = 4


stat_decay = 0.95
first_decay = 0.9
second_decay = 0.99
learning_rate = 0.5


def slot_of(owner_ref, block, capacity):
    rank = jnp.int32(0)
    for earlier in range(block):
        rank = rank + jnp.where(owner_ref[earlier] == owner_ref[block], 1, 0)
    return owner_ref[block] * capacity + rank


def send(source, target, send_sem, recv_sem, device):
    copy = pltpu.make_async_remote_copy(
        src_ref=source,
        dst_ref=target,
        send_sem=send_sem,
        recv_sem=recv_sem,
        device_id=device,
        device_id_type=pl.DeviceIdType.MESH,
    )
    copy.start()
    return copy


def greet(devices):
    barrier = pltpu.get_barrier_semaphore()
    for device in devices:
        pl.semaphore_signal(
            barrier, inc=1, device_id=device, device_id_type=pl.DeviceIdType.MESH
        )
    pl.semaphore_wait(barrier, len(devices))


def exchange(
    reps,
    owns,
    owner_ref,
    gradients_ref,
    summed_ref,
    raw,
    partial,
    arrived,
    same,
    other,
    local_sem,
    raw_send,
    raw_recv,
    own_send,
    own_recv,
    same_send,
    same_recv,
    other_send,
    other_recv,
):
    rep = lax.axis_index("rep")
    own = lax.axis_index("own")
    block_count = owner_ref.shape[0]
    capacity = summed_ref.shape[0]
    half = reps // 2

    def rep_device(target):
        return (target, own)

    def own_device(target):
        return (rep, target)

    mine = pltpu.make_async_copy(gradients_ref.at[:, rep], raw.at[0], local_sem)
    mine.start()
    greet(
        [rep_device(lax.rem(rep + step, reps)) for step in range(1, reps)]
        + [own_device(lax.rem(own + step, owns)) for step in range(1, owns)]
    )
    copies = []
    for step in range(1, reps):
        target = lax.rem(rep + step, reps)
        copies.append(
            send(
                gradients_ref.at[:, target],
                raw.at[step],
                raw_send.at[step],
                raw_recv.at[step],
                rep_device(target),
            )
        )
    slots = [slot_of(owner_ref, block, capacity) for block in range(block_count)]

    def source(slot):
        found = jnp.int32(0)
        for block in range(block_count):
            found = found + jnp.where(slots[block] == slot, block, 0)
        return found

    mine.wait()
    for copy in copies:
        copy.wait()

    copies = []
    for step in [*range(1, owns), 0]:
        target = lax.rem(own + step, owns)
        for place in range(capacity):
            block = source(target * capacity + place)
            total = raw[0, block].astype(jnp.float32)
            for peer in range(1, reps):
                total = total + raw[peer, block].astype(jnp.float32)
            partial[step, place] = total
        if step:
            copies.append(
                send(
                    partial.at[step],
                    arrived.at[step],
                    own_send.at[step],
                    own_recv.at[step],
                    own_device(target),
                )
            )
    for copy in copies:
        copy.wait()
    total = partial[0]
    for step in range(1, owns):
        total = total + arrived[step]
    same[0] = total

    high = lax.div(rep, 2)
    low = lax.rem(rep, 2)
    partner = rep_device(rep + 1 - 2 * low)
    first = []
    for step in range(1, half):
        target = lax.rem(high + step, half) * 2 + low
        first.append(
            send(
                same.at[0],
                same.at[step],
                same_send.at[step],
                same_recv.at[step],
                rep_device(target),
            )
        )
    second = [send(same.at[0], other.at[0], other_send.at[0], other_recv.at[0], partner)]
    for step in range(1, half):
        first[step - 1].wait_recv()
        second.append(
            send(
                same.at[step],
                other.at[step],
                other_send.at[step],
                other_recv.at[step],
                partner,
            )
        )
    for step in range(half):
        origin = lax.rem(high + half - step, half) * 2
        summed_ref[:, origin + low] = same[step]
        second[step].wait_recv()
        summed_ref[:, origin + 1 - low] = other[step]
    for copy in first + second:
        copy.wait_send()


def parts(value):
    upper = value.astype(jnp.bfloat16)
    lower = (value - upper.astype(jnp.float32)).astype(jnp.bfloat16)
    return upper, lower


def multiply(first, second, first_axis=1, second_axis=0):
    def dot(a, b):
        return lax.dot_general(
            a,
            b,
            (((first_axis,), (second_axis,)), ((), ())),
            preferred_element_type=jnp.float32,
        )

    return dot(first[0], second[0]) + (dot(first[0], second[1]) + dot(first[1], second[0]))


def refresh(
    row_count,
    owner_ref,
    summed_ref,
    left_ref,
    right_ref,
    left_root_ref,
    right_root_ref,
    first_ref,
    second_ref,
    master_ref,
    new_left_ref,
    new_right_ref,
    new_first_ref,
    new_second_ref,
    rows_ref,
    statistic,
    current,
    kept,
):
    capacity = left_ref.shape[0]
    block_size = left_ref.shape[-1]
    block_count = owner_ref.shape[0]
    rep = lax.axis_index("rep")
    own = lax.axis_index("own")
    slots = [slot_of(owner_ref, block, capacity) for block in range(block_count)]
    scale = (1.0 - stat_decay) / block_size

    for place in range(capacity):
        split = parts(summed_ref[place])
        statistic[place] = stat_decay * left_ref[place] + scale * multiply(split, split, 1, 1)
        statistic[capacity + place] = stat_decay * right_ref[place] + scale * multiply(
            split, split, 0, 0
        )
        current[place] = left_root_ref[place].astype(jnp.float32)
        current[capacity + place] = right_root_ref[place].astype(jnp.float32)

    chains = range(2 * capacity)

    def newton(iteration, carry):
        roots = [parts(current[chain]) for chain in chains]
        squares = [parts(multiply(roots[chain], roots[chain])) for chain in chains]
        fourths = [parts(multiply(squares[chain], squares[chain])) for chain in chains]
        residuals = [
            parts(multiply(fourths[chain], parts(statistic[chain]))) for chain in chains
        ]
        for chain in chains:
            current[chain] = (
                5.0 * current[chain] - multiply(roots[chain], residuals[chain])
            ) / 4.0
        return carry

    lax.fori_loop(0, NEWTON, newton, 0)

    def total(value):
        return jnp.sum(jnp.sum(value, axis=0, keepdims=True), axis=1, keepdims=True)

    for place in range(capacity):
        slot = own * capacity + place
        held = jnp.int32(0)
        for block in range(block_count):
            held = held + jnp.where(slots[block] == slot, 1, 0)
        summed = summed_ref[place]
        precond = multiply(
            parts(multiply(parts(current[place]), parts(summed))),
            parts(current[capacity + place]),
        )
        first_new = first_decay * first_ref[place] + (1.0 - first_decay) * summed
        second_new = second_decay * second_ref[place] + (1.0 - second_decay) * summed * summed
        adam_step = first_new / (jnp.sqrt(second_new) + 1e-08)
        graft = jnp.sqrt(total(adam_step * adam_step)) / (
            jnp.sqrt(total(precond * precond)) + 1e-06
        )
        kept[...] = precond
        start = pl.multiple_of(rep * row_count, row_count)
        rows = pl.ds(start, row_count)
        rows_ref[place] = (
            master_ref[place, rows, :] - learning_rate * graft * kept[rows, :]
        ).astype(jnp.bfloat16)

        @pl.when(held > 0)
        def _():
            new_left_ref[place] = statistic[place]
            new_right_ref[place] = statistic[capacity + place]
            new_first_ref[place] = first_new
            new_second_ref[place] = second_new

        @pl.when(held == 0)
        def _():
            new_left_ref[place] = left_ref[place]
            new_right_ref[place] = right_ref[place]
            new_first_ref[place] = first_ref[place]
            new_second_ref[place] = second_ref[place]


def share(owns, owner_ref, rows_ref, weights_ref, gathered, send_sem, recv_sem):
    rep = lax.axis_index("rep")
    own = lax.axis_index("own")
    block_count = owner_ref.shape[0]
    capacity = rows_ref.shape[0]
    targets = [(rep, lax.rem(own + step, owns)) for step in range(1, owns)]
    greet(targets)
    copies = [
        send(
            rows_ref,
            gathered.at[pl.ds(step * capacity, capacity)],
            send_sem.at[step],
            recv_sem.at[step],
            targets[step - 1],
        )
        for step in range(1, owns)
    ]
    gathered[0:capacity] = rows_ref[...]
    for copy in copies:
        copy.wait()
    for block in range(block_count):
        slot = slot_of(owner_ref, block, capacity)
        step = lax.rem(own + owns - owner_ref[block], owns)
        place = jnp.minimum(slot - owner_ref[block] * capacity, capacity - 1)
        weights_ref[block] = gathered[step * capacity + place]


def local(
    reps,
    owns,
    gradients,
    owner_index,
    left_stats,
    right_stats,
    left_roots,
    right_roots,
    first_moment,
    second_moment,
    master,
):
    capacity = left_stats.shape[0]
    block_size = left_stats.shape[-1]
    block_count = owner_index.shape[0]
    row_count = block_size // reps
    half = reps // 2
    vmem = pl.BlockSpec(memory_space=pltpu.VMEM)
    smem = pl.BlockSpec(memory_space=pltpu.SMEM)
    dma = pltpu.SemaphoreType.DMA
    piece = (capacity, row_count, block_size)

    summed = pl.pallas_call(
        functools.partial(exchange, reps, owns),
        out_shape=jax.ShapeDtypeStruct((capacity, reps, row_count, block_size), jnp.float32),
        in_specs=[smem, pl.BlockSpec(memory_space=pl.ANY)],
        out_specs=vmem,
        scratch_shapes=[
            pltpu.VMEM((reps, block_count, row_count, block_size), jnp.bfloat16),
            pltpu.VMEM((owns, *piece), jnp.float32),
            pltpu.VMEM((owns, *piece), jnp.float32),
            pltpu.VMEM((half, *piece), jnp.float32),
            pltpu.VMEM((half, *piece), jnp.float32),
            dma(()),
            dma((reps,)),
            dma((reps,)),
            dma((owns,)),
            dma((owns,)),
            dma((half,)),
            dma((half,)),
            dma((half,)),
            dma((half,)),
        ],
        compiler_params=pltpu.CompilerParams(
            collective_id=0, has_side_effects=True, vmem_limit_bytes=24 * 2**20
        ),
        name="exchange",
    )(owner_index, gradients.reshape(block_count, reps, row_count, block_size))
    summed = summed.reshape(capacity, block_size, block_size)

    full = jax.ShapeDtypeStruct((capacity, block_size, block_size), jnp.float32)
    new_left, new_right, new_first, new_second, rows = pl.pallas_call(
        functools.partial(refresh, row_count),
        out_shape=(full, full, full, full, jax.ShapeDtypeStruct(piece, jnp.bfloat16)),
        in_specs=[smem] + [vmem] * 8,
        out_specs=(vmem,) * 5,
        scratch_shapes=[
            pltpu.VMEM((2 * capacity, block_size, block_size), jnp.float32),
            pltpu.VMEM((2 * capacity, block_size, block_size), jnp.float32),
            pltpu.VMEM((block_size, block_size), jnp.float32),
        ],
        compiler_params=pltpu.CompilerParams(vmem_limit_bytes=24 * 2**20),
        name="refresh",
    )(
        owner_index,
        summed,
        left_stats,
        right_stats,
        left_roots,
        right_roots,
        first_moment,
        second_moment,
        master,
    )

    weights = pl.pallas_call(
        functools.partial(share, owns),
        out_shape=jax.ShapeDtypeStruct((block_count, row_count, block_size), jnp.bfloat16),
        in_specs=[smem, vmem],
        out_specs=vmem,
        scratch_shapes=[
            pltpu.VMEM((owns * capacity, row_count, block_size), jnp.bfloat16),
            dma((owns,)),
            dma((owns,)),
        ],
        compiler_params=pltpu.CompilerParams(
            collective_id=1, has_side_effects=True, vmem_limit_bytes=8 * 2**20
        ),
        name="share",
    )(owner_index, rows)
    return (new_left, new_right, new_first, new_second, weights)


def solution(mesh):
    return jax.shard_map(
        functools.partial(local, mesh.shape["rep"], mesh.shape["own"]),
        mesh=mesh,
        in_specs=(
            P("rep", "own", None, None, None),
            P(),
            P("own", None, None),
            P("own", None, None),
            P("own", None, None),
            P("own", None, None),
            P("own", None, None),
            P("own", None, None),
            P("own", None, None),
        ),
        out_specs=(
            P("own", None, None),
            P("own", None, None),
            P("own", None, None),
            P("own", None, None),
            P(None, "rep", None),
        ),
        check_vma=False,
    )
```

```python
import functools

import jax
import jax.numpy as jnp
from jax import lax
from jax.experimental import pallas as pl
from jax.experimental.pallas import tpu as pltpu
from jax.sharding import PartitionSpec as P

NEWTON = 4


stat_decay = 0.95
first_decay = 0.9
second_decay = 0.99
learning_rate = 0.5


def slot_of(owner_ref, block, capacity):
    rank = jnp.int32(0)
    for earlier in range(block):
        rank = rank + jnp.where(owner_ref[earlier] == owner_ref[block], 1, 0)
    return owner_ref[block] * capacity + rank


def send(source, target, send_sem, recv_sem, device):
    copy = pltpu.make_async_remote_copy(
        src_ref=source,
        dst_ref=target,
        send_sem=send_sem,
        recv_sem=recv_sem,
        device_id=device,
        device_id_type=pl.DeviceIdType.MESH,
    )
    copy.start()
    return copy


def greet(devices):
    barrier = pltpu.get_barrier_semaphore()
    for device in devices:
        pl.semaphore_signal(
            barrier, inc=1, device_id=device, device_id_type=pl.DeviceIdType.MESH
        )
    pl.semaphore_wait(barrier, len(devices))


def dot(first, second, first_axis=1, second_axis=0):
    return lax.dot_general(
        first,
        second,
        (((first_axis,), (second_axis,)), ((), ())),
        preferred_element_type=jnp.float32,
    )


def parts(value):
    upper = value.astype(jnp.bfloat16)
    lower = (value - upper.astype(jnp.float32)).astype(jnp.bfloat16)
    return upper, lower


def multiply(first, second, first_axis=1, second_axis=0):
    return dot(first[0], second[0], first_axis, second_axis) + (
        dot(first[0], second[1], first_axis, second_axis)
        + dot(first[1], second[0], first_axis, second_axis)
    )


def total(value):
    return jnp.sum(jnp.sum(value, axis=0, keepdims=True), axis=1, keepdims=True)


def step_kernel(
    reps,
    owns,
    chunks,
    owner_ref,
    gradients_ref,
    left_ref,
    right_ref,
    left_root_ref,
    right_root_ref,
    first_ref,
    second_ref,
    master_ref,
    new_left_ref,
    new_right_ref,
    new_first_ref,
    new_second_ref,
    weights_ref,
    raw,
    partial,
    arrived,
    same,
    other,
    summed,
    roots,
    statistics,
    first_in,
    second_in,
    master_in,
    fourth,
    upper,
    lower,
    current,
    kept,
    outgoing,
    gathered,
    load_sem,
    store_sem,
    mine_sem,
    raw_send,
    raw_recv,
    own_send,
    own_recv,
    same_send,
    same_recv,
    other_send,
    other_recv,
    row_send,
    row_recv,
):
    rep = lax.axis_index("rep")
    own = lax.axis_index("own")
    block_count = owner_ref.shape[0]
    capacity = new_left_ref.shape[0]
    block_size = new_left_ref.shape[-1]
    row_count = weights_ref.shape[1]
    piece_rows = row_count // chunks
    half = reps // 2
    chains = range(2 * capacity)

    def rep_device(target):
        return (target, own)

    def own_device(target):
        return (rep, target)

    loads = []
    for place, (source_ref, target_ref) in enumerate(
        (
            (left_root_ref, roots.at[0:capacity]),
            (right_root_ref, roots.at[capacity : 2 * capacity]),
            (left_ref, statistics.at[0:capacity]),
            (right_ref, statistics.at[capacity : 2 * capacity]),
            (first_ref, first_in),
            (second_ref, second_in),
            (master_ref, master_in),
        )
    ):
        loads.append(pltpu.make_async_copy(source_ref, target_ref, load_sem.at[place]))
        loads[-1].start()
    mine = []
    for chunk in range(chunks):
        mine.append(
            pltpu.make_async_copy(
                gradients_ref.at[:, rep * chunks + chunk], raw[chunk].at[0], mine_sem.at[chunk]
            )
        )
        mine[-1].start()
    greet(
        [rep_device(lax.rem(rep + step, reps)) for step in range(1, reps)]
        + [own_device(lax.rem(own + step, owns)) for step in range(1, owns)]
    )
    raw_copies = []
    for chunk in range(chunks):
        raw_copies.append([])
        for step in range(1, reps):
            target = lax.rem(rep + step, reps)
            raw_copies[-1].append(
                send(
                    gradients_ref.at[:, target * chunks + chunk],
                    raw[chunk].at[step],
                    raw_send.at[chunk, step],
                    raw_recv.at[chunk, step],
                    rep_device(target),
                )
            )
    slots = [slot_of(owner_ref, block, capacity) for block in range(block_count)]

    def source(slot):
        found = jnp.int32(0)
        for block in range(block_count):
            found = found + jnp.where(slots[block] == slot, block, 0)
        return found

    loads[0].wait()
    loads[1].wait()
    squares = [parts(dot(roots[chain], roots[chain])) for chain in chains]
    for chain in chains:
        fourth[chain] = multiply(squares[chain], squares[chain])

    own_copies = []
    for chunk in range(chunks):
        mine[chunk].wait()
        for copy in raw_copies[chunk]:
            copy.wait()
        own_copies.append([])
        for step in [*range(1, owns), 0]:
            target = lax.rem(own + step, owns)
            for place in range(capacity):
                block = source(target * capacity + place)
                value = raw[chunk][0, block].astype(jnp.float32)
                for peer in range(1, reps):
                    value = value + raw[chunk][peer, block].astype(jnp.float32)
                partial[chunk, step, place] = value
            if step:
                own_copies[-1].append(
                    send(
                        partial.at[chunk, step],
                        arrived.at[chunk, step],
                        own_send.at[chunk, step],
                        own_recv.at[chunk, step],
                        own_device(target),
                    )
                )

    high = lax.div(rep, 2)
    low = lax.rem(rep, 2)
    partner = rep_device(rep + 1 - 2 * low)
    first = []
    second = []
    for chunk in range(chunks):
        for copy in own_copies[chunk]:
            copy.wait()
        value = partial[chunk, 0]
        for step in range(1, owns):
            value = value + arrived[chunk, step]
        same[chunk, 0] = value
        first.append([])
        for step in range(1, half):
            target = lax.rem(high + step, half) * 2 + low
            first[-1].append(
                send(
                    same.at[chunk, 0],
                    same.at[chunk, step],
                    same_send.at[chunk, step],
                    same_recv.at[chunk, step],
                    rep_device(target),
                )
            )
        second.append(
            [
                send(
                    same.at[chunk, 0],
                    other.at[chunk, 0],
                    other_send.at[chunk, 0],
                    other_recv.at[chunk, 0],
                    partner,
                )
            ]
        )
    for chunk in range(chunks):
        for step in range(1, half):
            first[chunk][step - 1].wait_recv()
            second[chunk].append(
                send(
                    same.at[chunk, step],
                    other.at[chunk, step],
                    other_send.at[chunk, step],
                    other_recv.at[chunk, step],
                    partner,
                )
            )
    for copy in loads[2:]:
        copy.wait()
    for chunk in range(chunks):
        for step in range(half):
            origin = lax.rem(high + half - step, half) * 2
            second[chunk][step].wait_recv()
            for peer, held in ((origin + low, same), (origin + 1 - low, other)):
                start = pl.multiple_of(peer * row_count + chunk * piece_rows, piece_rows)
                summed[:, pl.ds(start, piece_rows), :] = held[chunk, step]

    scale = (1.0 - stat_decay) / block_size
    occupied = []
    for place in range(capacity):
        count = jnp.int32(0)
        for block in range(block_count):
            count = count + jnp.where(slots[block] == own * capacity + place, 1, 0)
        occupied.append(count > 0)
    adam_norms = []
    for place in range(capacity):
        gradient = summed[place]
        split = parts(gradient)
        for chain, axis in ((place, 1), (capacity + place, 0)):
            value = stat_decay * statistics[chain] + scale * multiply(split, split, axis, axis)
            upper[chain], lower[chain] = parts(value)
            statistics[chain] = jnp.where(occupied[place], value, statistics[chain])
        first_new = first_decay * first_in[place] + (1.0 - first_decay) * gradient
        second_new = second_decay * second_in[place] + (1.0 - second_decay) * gradient * gradient
        adam_step = first_new / (jnp.sqrt(second_new) + 1e-08)
        adam_norms.append(jnp.sqrt(total(adam_step * adam_step)))
        first_in[place] = jnp.where(occupied[place], first_new, first_in[place])
        second_in[place] = jnp.where(occupied[place], second_new, second_in[place])
    stores = []
    for place, (source_ref, target_ref) in enumerate(
        (
            (statistics.at[0:capacity], new_left_ref),
            (statistics.at[capacity : 2 * capacity], new_right_ref),
            (first_in, new_first_ref),
            (second_in, new_second_ref),
        )
    ):
        stores.append(pltpu.make_async_copy(source_ref, target_ref, store_sem.at[place]))
        stores[-1].start()

    def statistic(chain):
        return upper[chain], lower[chain]

    residuals = [parts(multiply(parts(fourth[chain]), statistic(chain))) for chain in chains]
    for chain in chains:
        initial = roots[chain]
        current[chain] = (
            5.0 * initial.astype(jnp.float32)
            - (dot(initial, residuals[chain][0]) + dot(initial, residuals[chain][1]))
        ) / 4.0

    def newton(iteration, carry):
        split = [parts(current[chain]) for chain in chains]
        squares = [parts(multiply(split[chain], split[chain])) for chain in chains]
        fourths = [parts(multiply(squares[chain], squares[chain])) for chain in chains]
        residuals = [parts(multiply(fourths[chain], statistic(chain))) for chain in chains]
        for chain in chains:
            current[chain] = (
                5.0 * current[chain] - multiply(split[chain], residuals[chain])
            ) / 4.0
        return carry

    lax.fori_loop(1, NEWTON, newton, 0)

    row_copies = []
    for place in range(capacity):
        gradient = summed[place]
        precond = multiply(
            parts(multiply(parts(current[place]), parts(gradient))),
            parts(current[capacity + place]),
        )
        graft = adam_norms[place] / (jnp.sqrt(total(precond * precond)) + 1e-06)
        kept[...] = precond
        rows = pl.ds(pl.multiple_of(rep * row_count, row_count), row_count)
        outgoing[place] = (
            master_in[place, rows, :] - learning_rate * graft * kept[rows, :]
        ).astype(jnp.bfloat16)
        for step in range(1, owns):
            row_copies.append(
                send(
                    outgoing.at[place],
                    gathered.at[step * capacity + place],
                    row_send.at[place, step],
                    row_recv.at[place, step],
                    own_device(lax.rem(own + step, owns)),
                )
            )
        gathered[place] = outgoing[place]
    for chunk in range(chunks):
        for copy in first[chunk] + second[chunk]:
            copy.wait_send()
    for copy in stores + row_copies:
        copy.wait()
    for block in range(block_count):
        step = lax.rem(own + owns - owner_ref[block], owns)
        place = jnp.minimum(slots[block] - owner_ref[block] * capacity, capacity - 1)
        weights_ref[block] = gathered[step * capacity + place]


def write(*refs):
    count = (len(refs) - 2) // 3
    loads = []
    stores = []
    for index in range(count):
        source_ref, target_ref, held = refs[index], refs[count + index], refs[2 * count + index]
        loads.append(pltpu.make_async_copy(source_ref, held, refs[-2].at[index]))
        stores.append(pltpu.make_async_copy(held, target_ref, refs[-1].at[index]))
        loads[-1].start()
    for load, store in zip(loads, stores):
        load.wait()
        store.start()
    for store in stores:
        store.wait()


def local(
    reps,
    owns,
    gradients,
    owner_index,
    left_stats,
    right_stats,
    left_roots,
    right_roots,
    first_moment,
    second_moment,
    master,
):
    capacity = left_stats.shape[0]
    block_size = left_stats.shape[-1]
    block_count = owner_index.shape[0]
    row_count = block_size // reps
    chunks = 2 if row_count % 32 == 0 else 1
    piece_rows = row_count // chunks
    half = reps // 2
    vmem = pl.BlockSpec(memory_space=pltpu.VMEM)
    smem = pl.BlockSpec(memory_space=pltpu.SMEM)
    hbm = pl.BlockSpec(memory_space=pltpu.HBM)
    dma = pltpu.SemaphoreType.DMA
    piece = (capacity, piece_rows, block_size)
    whole = (capacity, block_size, block_size)
    double = (2 * capacity, block_size, block_size)
    outputs = [jax.ShapeDtypeStruct(whole, jnp.float32)] * 4 + [
        jax.ShapeDtypeStruct((block_count, row_count, block_size), jnp.bfloat16)
    ]

    results = pl.pallas_call(
        functools.partial(step_kernel, reps, owns, chunks),
        out_shape=outputs,
        in_specs=[smem] + [hbm] * 8,
        out_specs=[hbm] * 4 + [vmem],
        scratch_shapes=[
            (pltpu.VMEM((reps, block_count, piece_rows, block_size), jnp.bfloat16),) * chunks,
            pltpu.VMEM((chunks, owns, *piece), jnp.float32),
            pltpu.VMEM((chunks, owns, *piece), jnp.float32),
            pltpu.VMEM((chunks, half, *piece), jnp.float32),
            pltpu.VMEM((chunks, half, *piece), jnp.float32),
            pltpu.VMEM(whole, jnp.float32),
            pltpu.VMEM(double, jnp.bfloat16),
            pltpu.VMEM(double, jnp.float32),
            pltpu.VMEM(whole, jnp.float32),
            pltpu.VMEM(whole, jnp.float32),
            pltpu.VMEM(whole, jnp.float32),
            pltpu.VMEM(double, jnp.float32),
            pltpu.VMEM(double, jnp.bfloat16),
            pltpu.VMEM(double, jnp.bfloat16),
            pltpu.VMEM(double, jnp.float32),
            pltpu.VMEM((block_size, block_size), jnp.float32),
            pltpu.VMEM((capacity, row_count, block_size), jnp.bfloat16),
            pltpu.VMEM((owns * capacity, row_count, block_size), jnp.bfloat16),
            dma((7,)),
            dma((4,)),
            dma((chunks,)),
            dma((chunks, reps)),
            dma((chunks, reps)),
            dma((chunks, owns)),
            dma((chunks, owns)),
            dma((chunks, half)),
            dma((chunks, half)),
            dma((chunks, half)),
            dma((chunks, half)),
            dma((capacity, owns)),
            dma((capacity, owns)),
        ],
        compiler_params=pltpu.CompilerParams(
            collective_id=0, has_side_effects=True, vmem_limit_bytes=247 * 2**18
        ),
        name="step",
    )(
        owner_index,
        gradients.reshape(block_count, reps * chunks, piece_rows, block_size),
        left_stats,
        right_stats,
        left_roots,
        right_roots,
        first_moment,
        second_moment,
        master,
    )
    return tuple(
        pl.pallas_call(
            write,
            out_shape=outputs,
            in_specs=[hbm] * 5,
            out_specs=[hbm] * 5,
            scratch_shapes=[pltpu.VMEM(leaf.shape, leaf.dtype) for leaf in outputs]
            + [dma((5,)), dma((5,))],
            compiler_params=pltpu.CompilerParams(vmem_limit_bytes=247 * 2**18),
            name="write",
        )(*results)
    )


def solution(mesh):
    return jax.shard_map(
        functools.partial(local, mesh.shape["rep"], mesh.shape["own"]),
        mesh=mesh,
        in_specs=(
            P("rep", "own", None, None, None),
            P(),
            P("own", None, None),
            P("own", None, None),
            P("own", None, None),
            P("own", None, None),
            P("own", None, None),
            P("own", None, None),
            P("own", None, None),
        ),
        out_specs=(
            P("own", None, None),
            P("own", None, None),
            P("own", None, None),
            P("own", None, None),
            P(None, "rep", None),
        ),
        check_vma=False,
    )
```

```python
import functools

import jax
import jax.numpy as jnp
from jax import lax
from jax.experimental import pallas as pl
from jax.experimental.pallas import tpu as pltpu
from jax.sharding import PartitionSpec as P

NEWTON = 4


stat_decay = 0.95
first_decay = 0.9
second_decay = 0.99
learning_rate = 0.5


def slot_of(owner_ref, block, capacity):
    rank = jnp.int32(0)
    for earlier in range(block):
        rank = rank + jnp.where(owner_ref[earlier] == owner_ref[block], 1, 0)
    return owner_ref[block] * capacity + rank


def send(source, target, send_sem, recv_sem, device):
    copy = pltpu.make_async_remote_copy(
        src_ref=source,
        dst_ref=target,
        send_sem=send_sem,
        recv_sem=recv_sem,
        device_id=device,
        device_id_type=pl.DeviceIdType.MESH,
    )
    copy.start()
    return copy


def greet(devices):
    barrier = pltpu.get_barrier_semaphore()
    for device in devices:
        pl.semaphore_signal(
            barrier, inc=1, device_id=device, device_id_type=pl.DeviceIdType.MESH
        )
    pl.semaphore_wait(barrier, len(devices))


def dot(first, second, first_axis=1, second_axis=0):
    return lax.dot_general(
        first,
        second,
        (((first_axis,), (second_axis,)), ((), ())),
        preferred_element_type=jnp.float32,
    )


def parts(value):
    upper = value.astype(jnp.bfloat16)
    lower = (value - upper.astype(jnp.float32)).astype(jnp.bfloat16)
    return upper, lower


def multiply(first, second, first_axis=1, second_axis=0):
    return dot(first[0], second[0], first_axis, second_axis) + (
        dot(first[0], second[1], first_axis, second_axis)
        + dot(first[1], second[0], first_axis, second_axis)
    )


def total(value):
    return jnp.sum(jnp.sum(value, axis=0, keepdims=True), axis=1, keepdims=True)


def step_kernel(
    reps,
    owns,
    chunks,
    owner_ref,
    gradients_ref,
    left_ref,
    right_ref,
    left_root_ref,
    right_root_ref,
    first_ref,
    second_ref,
    master_ref,
    new_left_ref,
    new_right_ref,
    new_first_ref,
    new_second_ref,
    weights_ref,
    raw,
    partial,
    arrived,
    same,
    other,
    summed,
    roots,
    statistics,
    first_in,
    second_in,
    master_in,
    fourth,
    upper,
    lower,
    current,
    kept,
    outgoing,
    gathered,
    load_sem,
    store_sem,
    mine_sem,
    raw_send,
    raw_recv,
    own_send,
    own_recv,
    same_send,
    same_recv,
    other_send,
    other_recv,
    row_send,
    row_recv,
    swap_send,
    swap_recv,
):
    rep = lax.axis_index("rep")
    own = lax.axis_index("own")
    block_count = owner_ref.shape[0]
    capacity = new_left_ref.shape[0]
    block_size = new_left_ref.shape[-1]
    row_count = weights_ref.shape[1]
    piece_rows = row_count // chunks
    half = reps // 2
    places = range(capacity)
    high = lax.div(rep, 2)
    low = lax.rem(rep, 2)

    def rep_device(target):
        return (target, own)

    def own_device(target):
        return (rep, target)

    partner = rep_device(rep + 1 - 2 * low)

    def chain(place):
        return low * capacity + place

    loads = []
    for place, (source_ref, target_ref) in enumerate(
        (
            (left_root_ref, roots.at[0:capacity]),
            (right_root_ref, roots.at[capacity : 2 * capacity]),
            (left_ref, statistics.at[0:capacity]),
            (right_ref, statistics.at[capacity : 2 * capacity]),
            (first_ref, first_in),
            (second_ref, second_in),
            (master_ref, master_in),
        )
    ):
        loads.append(pltpu.make_async_copy(source_ref, target_ref, load_sem.at[place]))
        loads[-1].start()
    mine = []
    for chunk in range(chunks):
        mine.append(
            pltpu.make_async_copy(
                gradients_ref.at[:, rep * chunks + chunk], raw[chunk].at[0], mine_sem.at[chunk]
            )
        )
        mine[-1].start()
    greet(
        [rep_device(lax.rem(rep + step, reps)) for step in range(1, reps)]
        + [own_device(lax.rem(own + step, owns)) for step in range(1, owns)]
    )
    raw_copies = []
    for chunk in range(chunks):
        raw_copies.append([])
        for step in range(1, reps):
            target = lax.rem(rep + step, reps)
            raw_copies[-1].append(
                send(
                    gradients_ref.at[:, target * chunks + chunk],
                    raw[chunk].at[step],
                    raw_send.at[chunk, step],
                    raw_recv.at[chunk, step],
                    rep_device(target),
                )
            )
    slots = [slot_of(owner_ref, block, capacity) for block in range(block_count)]

    def source(slot):
        found = jnp.int32(0)
        for block in range(block_count):
            found = found + jnp.where(slots[block] == slot, block, 0)
        return found

    loads[0].wait()
    loads[1].wait()
    squares = [parts(dot(roots[chain(place)], roots[chain(place)])) for place in places]
    for place in places:
        fourth[place] = multiply(squares[place], squares[place])

    own_copies = []
    for chunk in range(chunks):
        mine[chunk].wait()
        for copy in raw_copies[chunk]:
            copy.wait()
        own_copies.append([])
        for step in [*range(1, owns), 0]:
            target = lax.rem(own + step, owns)
            for place in range(capacity):
                block = source(target * capacity + place)
                value = raw[chunk][0, block].astype(jnp.float32)
                for peer in range(1, reps):
                    value = value + raw[chunk][peer, block].astype(jnp.float32)
                partial[chunk, step, place] = value
            if step:
                own_copies[-1].append(
                    send(
                        partial.at[chunk, step],
                        arrived.at[chunk, step],
                        own_send.at[chunk, step],
                        own_recv.at[chunk, step],
                        own_device(target),
                    )
                )

    first = []
    second = []
    for chunk in range(chunks):
        for copy in own_copies[chunk]:
            copy.wait()
        value = partial[chunk, 0]
        for step in range(1, owns):
            value = value + arrived[chunk, step]
        same[chunk, 0] = value
        first.append([])
        for step in range(1, half):
            target = lax.rem(high + step, half) * 2 + low
            first[-1].append(
                send(
                    same.at[chunk, 0],
                    same.at[chunk, step],
                    same_send.at[chunk, step],
                    same_recv.at[chunk, step],
                    rep_device(target),
                )
            )
        second.append(
            [
                send(
                    same.at[chunk, 0],
                    other.at[chunk, 0],
                    other_send.at[chunk, 0],
                    other_recv.at[chunk, 0],
                    partner,
                )
            ]
        )
    for chunk in range(chunks):
        for step in range(1, half):
            first[chunk][step - 1].wait_recv()
            second[chunk].append(
                send(
                    same.at[chunk, step],
                    other.at[chunk, step],
                    other_send.at[chunk, step],
                    other_recv.at[chunk, step],
                    partner,
                )
            )
    for copy in loads[2:]:
        copy.wait()
    for chunk in range(chunks):
        for step in range(half):
            origin = lax.rem(high + half - step, half) * 2
            second[chunk][step].wait_recv()
            for peer, held in ((origin + low, same), (origin + 1 - low, other)):
                start = pl.multiple_of(peer * row_count + chunk * piece_rows, piece_rows)
                summed[:, pl.ds(start, piece_rows), :] = held[chunk, step]

    scale = (1.0 - stat_decay) / block_size
    occupied = []
    for place in range(capacity):
        count = jnp.int32(0)
        for block in range(block_count):
            count = count + jnp.where(slots[block] == own * capacity + place, 1, 0)
        occupied.append(count > 0)

    stores = [
        pltpu.make_async_copy(source_ref, target_ref, store_sem.at[place])
        for place, (source_ref, target_ref) in enumerate(
            (
                (statistics.at[0:capacity], new_left_ref),
                (statistics.at[capacity : 2 * capacity], new_right_ref),
                (first_in, new_first_ref),
                (second_in, new_second_ref),
            )
        )
    ]

    def left_statistic(place):
        split = parts(summed[place])
        return stat_decay * statistics[place] + scale * multiply(split, split, 1, 1)

    def right_statistic(place):
        split = parts(summed[place])
        return stat_decay * statistics[capacity + place] + scale * multiply(split, split, 0, 0)

    @pl.when(low == 0)
    def _():
        for place in places:
            value = left_statistic(place)
            upper[place], lower[place] = parts(value)
            statistics[place] = jnp.where(occupied[place], value, statistics[place])

    @pl.when(low == 1)
    def _():
        for place in places:
            value = right_statistic(place)
            upper[place], lower[place] = parts(value)
            statistics[capacity + place] = jnp.where(
                occupied[place], value, statistics[capacity + place]
            )

    def statistic(place):
        return upper[place], lower[place]

    residuals = [parts(multiply(parts(fourth[place]), statistic(place))) for place in places]
    for place in places:
        initial = roots[chain(place)]
        current[chain(place)] = (
            5.0 * initial.astype(jnp.float32)
            - (dot(initial, residuals[place][0]) + dot(initial, residuals[place][1]))
        ) / 4.0

    def newton(iteration, carry):
        split = [parts(current[chain(place)]) for place in places]
        squares = [parts(multiply(split[place], split[place])) for place in places]
        fourths = [parts(multiply(squares[place], squares[place])) for place in places]
        residuals = [parts(multiply(fourths[place], statistic(place))) for place in places]
        for place in places:
            current[chain(place)] = (
                5.0 * current[chain(place)] - multiply(split[place], residuals[place])
            ) / 4.0
        return carry

    lax.fori_loop(1, NEWTON, newton, 0)

    swaps = [
        send(
            current.at[chain(place)],
            current.at[chain(place)],
            swap_send.at[place],
            swap_recv.at[place],
            partner,
        )
        for place in places
    ]

    @pl.when(low == 1)
    def _():
        for place in places:
            statistics[place] = jnp.where(
                occupied[place], left_statistic(place), statistics[place]
            )

    @pl.when(low == 0)
    def _():
        for place in places:
            statistics[capacity + place] = jnp.where(
                occupied[place], right_statistic(place), statistics[capacity + place]
            )

    adam_norms = []
    for place in places:
        gradient = summed[place]
        first_new = first_decay * first_in[place] + (1.0 - first_decay) * gradient
        second_new = second_decay * second_in[place] + (1.0 - second_decay) * gradient * gradient
        adam_step = first_new / (jnp.sqrt(second_new) + 1e-08)
        adam_norms.append(jnp.sqrt(total(adam_step * adam_step)))
        first_in[place] = jnp.where(occupied[place], first_new, first_in[place])
        second_in[place] = jnp.where(occupied[place], second_new, second_in[place])
    for store in stores:
        store.start()

    row_copies = []
    for place in range(capacity):
        swaps[place].wait()
        precond = multiply(
            parts(multiply(parts(current[place]), parts(summed[place]))),
            parts(current[capacity + place]),
        )
        graft = adam_norms[place] / (jnp.sqrt(total(precond * precond)) + 1e-06)
        kept[...] = precond
        rows = pl.ds(pl.multiple_of(rep * row_count, row_count), row_count)
        outgoing[place] = (
            master_in[place, rows, :] - learning_rate * graft * kept[rows, :]
        ).astype(jnp.bfloat16)
        for step in range(1, owns):
            row_copies.append(
                send(
                    outgoing.at[place],
                    gathered.at[step * capacity + place],
                    row_send.at[place, step],
                    row_recv.at[place, step],
                    own_device(lax.rem(own + step, owns)),
                )
            )
        gathered[place] = outgoing[place]
    for chunk in range(chunks):
        for copy in first[chunk] + second[chunk]:
            copy.wait_send()
    for copy in stores + row_copies:
        copy.wait()
    for block in range(block_count):
        step = lax.rem(own + owns - owner_ref[block], owns)
        place = jnp.minimum(slots[block] - owner_ref[block] * capacity, capacity - 1)
        weights_ref[block] = gathered[step * capacity + place]


def write(*refs):
    count = (len(refs) - 2) // 3
    loads = []
    stores = []
    for index in range(count):
        source_ref, target_ref, held = refs[index], refs[count + index], refs[2 * count + index]
        loads.append(pltpu.make_async_copy(source_ref, held, refs[-2].at[index]))
        stores.append(pltpu.make_async_copy(held, target_ref, refs[-1].at[index]))
        loads[-1].start()
    for load, store in zip(loads, stores):
        load.wait()
        store.start()
    for store in stores:
        store.wait()


def local(
    reps,
    owns,
    gradients,
    owner_index,
    left_stats,
    right_stats,
    left_roots,
    right_roots,
    first_moment,
    second_moment,
    master,
):
    capacity = left_stats.shape[0]
    block_size = left_stats.shape[-1]
    block_count = owner_index.shape[0]
    row_count = block_size // reps
    chunks = 4 if row_count % 32 == 0 else 1
    piece_rows = row_count // chunks
    half = reps // 2
    vmem = pl.BlockSpec(memory_space=pltpu.VMEM)
    smem = pl.BlockSpec(memory_space=pltpu.SMEM)
    hbm = pl.BlockSpec(memory_space=pltpu.HBM)
    dma = pltpu.SemaphoreType.DMA
    piece = (capacity, piece_rows, block_size)
    whole = (capacity, block_size, block_size)
    double = (2 * capacity, block_size, block_size)
    outputs = [jax.ShapeDtypeStruct(whole, jnp.float32)] * 4 + [
        jax.ShapeDtypeStruct((block_count, row_count, block_size), jnp.bfloat16)
    ]

    results = pl.pallas_call(
        functools.partial(step_kernel, reps, owns, chunks),
        out_shape=outputs,
        in_specs=[smem] + [hbm] * 8,
        out_specs=[hbm] * 4 + [vmem],
        scratch_shapes=[
            (pltpu.VMEM((reps, block_count, piece_rows, block_size), jnp.bfloat16),) * chunks,
            pltpu.VMEM((chunks, owns, *piece), jnp.float32),
            pltpu.VMEM((chunks, owns, *piece), jnp.float32),
            pltpu.VMEM((chunks, half, *piece), jnp.float32),
            pltpu.VMEM((chunks, half, *piece), jnp.float32),
            pltpu.VMEM(whole, jnp.float32),
            pltpu.VMEM(double, jnp.bfloat16),
            pltpu.VMEM(double, jnp.float32),
            pltpu.VMEM(whole, jnp.float32),
            pltpu.VMEM(whole, jnp.float32),
            pltpu.VMEM(whole, jnp.float32),
            pltpu.VMEM(whole, jnp.float32),
            pltpu.VMEM(whole, jnp.bfloat16),
            pltpu.VMEM(whole, jnp.bfloat16),
            pltpu.VMEM(double, jnp.float32),
            pltpu.VMEM((block_size, block_size), jnp.float32),
            pltpu.VMEM((capacity, row_count, block_size), jnp.bfloat16),
            pltpu.VMEM((owns * capacity, row_count, block_size), jnp.bfloat16),
            dma((7,)),
            dma((4,)),
            dma((chunks,)),
            dma((chunks, reps)),
            dma((chunks, reps)),
            dma((chunks, owns)),
            dma((chunks, owns)),
            dma((chunks, half)),
            dma((chunks, half)),
            dma((chunks, half)),
            dma((chunks, half)),
            dma((capacity, owns)),
            dma((capacity, owns)),
            dma((capacity,)),
            dma((capacity,)),
        ],
        compiler_params=pltpu.CompilerParams(
            collective_id=0, has_side_effects=True, vmem_limit_bytes=247 * 2**18
        ),
        name="step",
    )(
        owner_index,
        gradients.reshape(block_count, reps * chunks, piece_rows, block_size),
        left_stats,
        right_stats,
        left_roots,
        right_roots,
        first_moment,
        second_moment,
        master,
    )
    return tuple(
        pl.pallas_call(
            write,
            out_shape=outputs,
            in_specs=[hbm] * 5,
            out_specs=[hbm] * 5,
            scratch_shapes=[pltpu.VMEM(leaf.shape, leaf.dtype) for leaf in outputs]
            + [dma((5,)), dma((5,))],
            compiler_params=pltpu.CompilerParams(vmem_limit_bytes=247 * 2**18),
            name="write",
        )(*results)
    )


def solution(mesh):
    return jax.shard_map(
        functools.partial(local, mesh.shape["rep"], mesh.shape["own"]),
        mesh=mesh,
        in_specs=(
            P("rep", "own", None, None, None),
            P(),
            P("own", None, None),
            P("own", None, None),
            P("own", None, None),
            P("own", None, None),
            P("own", None, None),
            P("own", None, None),
            P("own", None, None),
        ),
        out_specs=(
            P("own", None, None),
            P("own", None, None),
            P("own", None, None),
            P("own", None, None),
            P(None, "rep", None),
        ),
        check_vma=False,
    )
```

```python
import functools

import jax
import jax.numpy as jnp
from jax import lax
from jax.experimental import pallas as pl
from jax.experimental.pallas import tpu as pltpu
from jax.sharding import PartitionSpec as P

NEWTON = 4


stat_decay = 0.95
first_decay = 0.9
second_decay = 0.99
learning_rate = 0.5


def slot_of(owner_ref, block, capacity):
    rank = jnp.int32(0)
    for earlier in range(block):
        rank = rank + jnp.where(owner_ref[earlier] == owner_ref[block], 1, 0)
    return owner_ref[block] * capacity + rank


def send(source, target, send_sem, recv_sem, device):
    copy = pltpu.make_async_remote_copy(
        src_ref=source,
        dst_ref=target,
        send_sem=send_sem,
        recv_sem=recv_sem,
        device_id=device,
        device_id_type=pl.DeviceIdType.MESH,
    )
    copy.start()
    return copy


def greet(devices):
    barrier = pltpu.get_barrier_semaphore()
    for device in devices:
        pl.semaphore_signal(
            barrier, inc=1, device_id=device, device_id_type=pl.DeviceIdType.MESH
        )
    pl.semaphore_wait(barrier, len(devices))


def dot(first, second, first_axis=1, second_axis=0):
    return lax.dot_general(
        first,
        second,
        (((first_axis,), (second_axis,)), ((), ())),
        preferred_element_type=jnp.float32,
    )


def parts(value):
    upper = value.astype(jnp.bfloat16)
    lower = (value - upper.astype(jnp.float32)).astype(jnp.bfloat16)
    return upper, lower


def multiply(first, second, first_axis=1, second_axis=0):
    return dot(first[0], second[0], first_axis, second_axis) + (
        dot(first[0], second[1], first_axis, second_axis)
        + dot(first[1], second[0], first_axis, second_axis)
    )


def total(value):
    return jnp.sum(jnp.sum(value, axis=0, keepdims=True), axis=1, keepdims=True)


def step_kernel(
    reps,
    owns,
    chunks,
    owner_ref,
    gradients_ref,
    left_ref,
    right_ref,
    left_root_ref,
    right_root_ref,
    first_ref,
    second_ref,
    master_ref,
    new_left_ref,
    new_right_ref,
    new_first_ref,
    new_second_ref,
    weights_ref,
    raw,
    partial,
    arrived,
    same,
    other,
    summed,
    roots,
    statistics,
    first_in,
    second_in,
    master_in,
    fourth,
    upper,
    lower,
    current,
    kept,
    outgoing,
    gathered,
    load_sem,
    store_sem,
    mine_sem,
    raw_send,
    raw_recv,
    own_send,
    own_recv,
    same_send,
    same_recv,
    other_send,
    other_recv,
    row_send,
    row_recv,
    swap_send,
    swap_recv,
):
    rep = lax.axis_index("rep")
    own = lax.axis_index("own")
    block_count = owner_ref.shape[0]
    capacity = new_left_ref.shape[0]
    block_size = new_left_ref.shape[-1]
    row_count = weights_ref.shape[1]
    piece_rows = row_count // chunks
    half = reps // 2
    places = range(capacity)
    high = lax.div(rep, 2)
    low = lax.rem(rep, 2)

    def rep_device(target):
        return (target, own)

    def own_device(target):
        return (rep, target)

    partner = rep_device(rep + 1 - 2 * low)

    def chain(place):
        return low * capacity + place

    loads = []
    for place, (source_ref, target_ref) in enumerate(
        (
            (left_root_ref, roots.at[0:capacity]),
            (right_root_ref, roots.at[capacity : 2 * capacity]),
            (left_ref, statistics.at[0:capacity]),
            (right_ref, statistics.at[capacity : 2 * capacity]),
            (first_ref, first_in),
            (second_ref, second_in),
            (master_ref, master_in),
        )
    ):
        loads.append(pltpu.make_async_copy(source_ref, target_ref, load_sem.at[place]))
        loads[-1].start()
    mine = []
    for chunk in range(chunks):
        mine.append(
            pltpu.make_async_copy(
                gradients_ref.at[:, rep * chunks + chunk], raw[chunk].at[0], mine_sem.at[chunk]
            )
        )
        mine[-1].start()
    greet(
        [rep_device(lax.rem(rep + step, reps)) for step in range(1, reps)]
        + [own_device(lax.rem(own + step, owns)) for step in range(1, owns)]
    )
    raw_copies = []
    for chunk in range(chunks):
        raw_copies.append([])
        for step in range(1, reps):
            target = lax.rem(rep + step, reps)
            raw_copies[-1].append(
                send(
                    gradients_ref.at[:, target * chunks + chunk],
                    raw[chunk].at[step],
                    raw_send.at[chunk, step],
                    raw_recv.at[chunk, step],
                    rep_device(target),
                )
            )
    slots = [slot_of(owner_ref, block, capacity) for block in range(block_count)]

    def source(slot):
        found = jnp.int32(0)
        for block in range(block_count):
            found = found + jnp.where(slots[block] == slot, block, 0)
        return found

    loads[0].wait()
    loads[1].wait()
    squares = [parts(dot(roots[chain(place)], roots[chain(place)])) for place in places]
    for place in places:
        fourth[place] = multiply(squares[place], squares[place])

    own_copies = []
    for chunk in range(chunks):
        mine[chunk].wait()
        for copy in raw_copies[chunk]:
            copy.wait()
        own_copies.append([])
        for step in [*range(1, owns), 0]:
            target = lax.rem(own + step, owns)
            for place in range(capacity):
                block = source(target * capacity + place)
                value = raw[chunk][0, block].astype(jnp.float32)
                for peer in range(1, reps):
                    value = value + raw[chunk][peer, block].astype(jnp.float32)
                partial[chunk, step, place] = value
            if step:
                own_copies[-1].append(
                    send(
                        partial.at[chunk, step],
                        arrived.at[chunk, step],
                        own_send.at[chunk, step],
                        own_recv.at[chunk, step],
                        own_device(target),
                    )
                )

    first = []
    second = []
    for chunk in range(chunks):
        for copy in own_copies[chunk]:
            copy.wait()
        value = partial[chunk, 0]
        for step in range(1, owns):
            value = value + arrived[chunk, step]
        same[chunk, 0] = value
        first.append([])
        for step in range(1, half):
            target = lax.rem(high + step, half) * 2 + low
            first[-1].append(
                send(
                    same.at[chunk, 0],
                    same.at[chunk, step],
                    same_send.at[chunk, step],
                    same_recv.at[chunk, step],
                    rep_device(target),
                )
            )
        second.append(
            [
                send(
                    same.at[chunk, 0],
                    other.at[chunk, 0],
                    other_send.at[chunk, 0],
                    other_recv.at[chunk, 0],
                    partner,
                )
            ]
        )
    for chunk in range(chunks):
        for step in range(1, half):
            first[chunk][step - 1].wait_recv()
            second[chunk].append(
                send(
                    same.at[chunk, step],
                    other.at[chunk, step],
                    other_send.at[chunk, step],
                    other_recv.at[chunk, step],
                    partner,
                )
            )
    for copy in loads[2:]:
        copy.wait()
    for chunk in range(chunks):
        for step in range(half):
            origin = lax.rem(high + half - step, half) * 2
            second[chunk][step].wait_recv()
            for peer, held in ((origin + low, same), (origin + 1 - low, other)):
                start = pl.multiple_of(peer * row_count + chunk * piece_rows, piece_rows)
                summed[:, pl.ds(start, piece_rows), :] = held[chunk, step]

    scale = (1.0 - stat_decay) / block_size
    occupied = []
    for place in range(capacity):
        count = jnp.int32(0)
        for block in range(block_count):
            count = count + jnp.where(slots[block] == own * capacity + place, 1, 0)
        occupied.append(count > 0)

    stores = [
        pltpu.make_async_copy(source_ref, target_ref, store_sem.at[place])
        for place, (source_ref, target_ref) in enumerate(
            (
                (statistics.at[0:capacity], new_left_ref),
                (statistics.at[capacity : 2 * capacity], new_right_ref),
                (first_in, new_first_ref),
                (second_in, new_second_ref),
            )
        )
    ]

    def left_statistic(place):
        split = parts(summed[place])
        return stat_decay * statistics[place] + scale * multiply(split, split, 1, 1)

    def right_statistic(place):
        split = parts(summed[place])
        return stat_decay * statistics[capacity + place] + scale * multiply(split, split, 0, 0)

    @pl.when(low == 0)
    def _():
        for place in places:
            value = left_statistic(place)
            upper[place], lower[place] = parts(value)
            statistics[place] = jnp.where(occupied[place], value, statistics[place])

    @pl.when(low == 1)
    def _():
        for place in places:
            value = right_statistic(place)
            upper[place], lower[place] = parts(value)
            statistics[capacity + place] = jnp.where(
                occupied[place], value, statistics[capacity + place]
            )

    def statistic(place):
        return upper[place], lower[place]

    residuals = [parts(multiply(parts(fourth[place]), statistic(place))) for place in places]
    for place in places:
        initial = roots[chain(place)]
        current[chain(place)] = (
            5.0 * initial.astype(jnp.float32)
            - (dot(initial, residuals[place][0]) + dot(initial, residuals[place][1]))
        ) / 4.0

    def newton(iteration, carry):
        split = [parts(current[chain(place)]) for place in places]
        squares = [parts(multiply(split[place], split[place])) for place in places]
        fourths = [parts(multiply(squares[place], squares[place])) for place in places]
        residuals = [parts(multiply(fourths[place], statistic(place))) for place in places]
        for place in places:
            current[chain(place)] = (
                5.0 * current[chain(place)] - multiply(split[place], residuals[place])
            ) / 4.0
        return carry

    lax.fori_loop(1, NEWTON, newton, 0)

    @pl.when(low == 0)
    def _():
        for place in places:
            current[place] = multiply(parts(current[place]), parts(summed[place]))

    swaps = [
        send(
            current.at[chain(place)],
            current.at[chain(place)],
            swap_send.at[place],
            swap_recv.at[place],
            partner,
        )
        for place in places
    ]

    @pl.when(low == 1)
    def _():
        for place in places:
            statistics[place] = jnp.where(
                occupied[place], left_statistic(place), statistics[place]
            )

    @pl.when(low == 0)
    def _():
        for place in places:
            statistics[capacity + place] = jnp.where(
                occupied[place], right_statistic(place), statistics[capacity + place]
            )

    adam_norms = []
    for place in places:
        gradient = summed[place]
        first_new = first_decay * first_in[place] + (1.0 - first_decay) * gradient
        second_new = second_decay * second_in[place] + (1.0 - second_decay) * gradient * gradient
        adam_step = first_new / (jnp.sqrt(second_new) + 1e-08)
        adam_norms.append(jnp.sqrt(total(adam_step * adam_step)))
        first_in[place] = jnp.where(occupied[place], first_new, first_in[place])
        second_in[place] = jnp.where(occupied[place], second_new, second_in[place])
    for store in stores:
        store.start()

    row_copies = []
    for place in range(capacity):
        swaps[place].wait()
        precond = multiply(parts(current[place]), parts(current[capacity + place]))
        graft = adam_norms[place] / (jnp.sqrt(total(precond * precond)) + 1e-06)
        kept[...] = precond
        rows = pl.ds(pl.multiple_of(rep * row_count, row_count), row_count)
        outgoing[place] = (
            master_in[place, rows, :] - learning_rate * graft * kept[rows, :]
        ).astype(jnp.bfloat16)
        for step in range(1, owns):
            row_copies.append(
                send(
                    outgoing.at[place],
                    gathered.at[step * capacity + place],
                    row_send.at[place, step],
                    row_recv.at[place, step],
                    own_device(lax.rem(own + step, owns)),
                )
            )
        gathered[place] = outgoing[place]
    for chunk in range(chunks):
        for copy in first[chunk] + second[chunk]:
            copy.wait_send()
    for copy in stores + row_copies:
        copy.wait()
    for block in range(block_count):
        step = lax.rem(own + owns - owner_ref[block], owns)
        place = jnp.minimum(slots[block] - owner_ref[block] * capacity, capacity - 1)
        weights_ref[block] = gathered[step * capacity + place]


def write(*refs):
    count = (len(refs) - 2) // 3
    loads = []
    stores = []
    for index in range(count):
        source_ref, target_ref, held = refs[index], refs[count + index], refs[2 * count + index]
        for part in range(source_ref.shape[0]):
            loads.append(
                pltpu.make_async_copy(source_ref.at[part], held.at[part], refs[-2].at[index, part])
            )
            stores.append(
                pltpu.make_async_copy(held.at[part], target_ref.at[part], refs[-1].at[index, part])
            )
            loads[-1].start()
    for load, store in zip(loads, stores):
        load.wait()
        store.start()
    for store in stores:
        store.wait()


def local(
    reps,
    owns,
    gradients,
    owner_index,
    left_stats,
    right_stats,
    left_roots,
    right_roots,
    first_moment,
    second_moment,
    master,
):
    capacity = left_stats.shape[0]
    block_size = left_stats.shape[-1]
    block_count = owner_index.shape[0]
    row_count = block_size // reps
    chunks = 4 if row_count % 32 == 0 else 1
    piece_rows = row_count // chunks
    half = reps // 2
    vmem = pl.BlockSpec(memory_space=pltpu.VMEM)
    smem = pl.BlockSpec(memory_space=pltpu.SMEM)
    hbm = pl.BlockSpec(memory_space=pltpu.HBM)
    dma = pltpu.SemaphoreType.DMA
    piece = (capacity, piece_rows, block_size)
    whole = (capacity, block_size, block_size)
    double = (2 * capacity, block_size, block_size)
    outputs = [jax.ShapeDtypeStruct(whole, jnp.float32)] * 4 + [
        jax.ShapeDtypeStruct((block_count, row_count, block_size), jnp.bfloat16)
    ]

    results = pl.pallas_call(
        functools.partial(step_kernel, reps, owns, chunks),
        out_shape=outputs,
        in_specs=[smem] + [hbm] * 8,
        out_specs=[hbm] * 4 + [vmem],
        scratch_shapes=[
            (pltpu.VMEM((reps, block_count, piece_rows, block_size), jnp.bfloat16),) * chunks,
            pltpu.VMEM((chunks, owns, *piece), jnp.float32),
            pltpu.VMEM((chunks, owns, *piece), jnp.float32),
            pltpu.VMEM((chunks, half, *piece), jnp.float32),
            pltpu.VMEM((chunks, half, *piece), jnp.float32),
            pltpu.VMEM(whole, jnp.float32),
            pltpu.VMEM(double, jnp.bfloat16),
            pltpu.VMEM(double, jnp.float32),
            pltpu.VMEM(whole, jnp.float32),
            pltpu.VMEM(whole, jnp.float32),
            pltpu.VMEM(whole, jnp.float32),
            pltpu.VMEM(whole, jnp.float32),
            pltpu.VMEM(whole, jnp.bfloat16),
            pltpu.VMEM(whole, jnp.bfloat16),
            pltpu.VMEM(double, jnp.float32),
            pltpu.VMEM((block_size, block_size), jnp.float32),
            pltpu.VMEM((capacity, row_count, block_size), jnp.bfloat16),
            pltpu.VMEM((owns * capacity, row_count, block_size), jnp.bfloat16),
            dma((7,)),
            dma((4,)),
            dma((chunks,)),
            dma((chunks, reps)),
            dma((chunks, reps)),
            dma((chunks, owns)),
            dma((chunks, owns)),
            dma((chunks, half)),
            dma((chunks, half)),
            dma((chunks, half)),
            dma((chunks, half)),
            dma((capacity, owns)),
            dma((capacity, owns)),
            dma((capacity,)),
            dma((capacity,)),
        ],
        compiler_params=pltpu.CompilerParams(
            collective_id=0, has_side_effects=True, vmem_limit_bytes=247 * 2**18
        ),
        name="step",
    )(
        owner_index,
        gradients.reshape(block_count, reps * chunks, piece_rows, block_size),
        left_stats,
        right_stats,
        left_roots,
        right_roots,
        first_moment,
        second_moment,
        master,
    )
    return tuple(
        pl.pallas_call(
            write,
            out_shape=outputs,
            in_specs=[hbm] * 5,
            out_specs=[hbm] * 5,
            scratch_shapes=[pltpu.VMEM(leaf.shape, leaf.dtype) for leaf in outputs]
            + [dma((5, max(capacity, block_count)))] * 2,
            compiler_params=pltpu.CompilerParams(vmem_limit_bytes=247 * 2**18),
            name="write",
        )(*results)
    )


def solution(mesh):
    return jax.shard_map(
        functools.partial(local, mesh.shape["rep"], mesh.shape["own"]),
        mesh=mesh,
        in_specs=(
            P("rep", "own", None, None, None),
            P(),
            P("own", None, None),
            P("own", None, None),
            P("own", None, None),
            P("own", None, None),
            P("own", None, None),
            P("own", None, None),
            P("own", None, None),
        ),
        out_specs=(
            P("own", None, None),
            P("own", None, None),
            P("own", None, None),
            P("own", None, None),
            P(None, "rep", None),
        ),
        check_vma=False,
    )
```
